32 devices in a mesh: dp: 4 (over z), mp: 8 (over y, x, core).
Axes of the slice: x: 2, y: 2, z: 4, core: 2. Of those that a mesh axis runs over, the one named last changes fastest.
Arguments:
- accumulated: bfloat16 [4, 14336, 4096], P('dp', 'mp'), may hold values from -6 to 6
- start_q: float32 [4096, 128], replicated, may hold values from -6 to 6
Outputs:
- update: float32 [14336, 4096], P('mp')
- new_error: bfloat16 [4, 14336, 4096], P('dp', 'mp')
The draws below stay inside these ranges and needn't reach their ends.
All inputs are finite; a program needn't handle non-finite values.
Results may differ from the reference program's by a relative error of at most 0.0059.
Values sent between devices are 32-bit elements; how exact they have to be, the bound alone decides.
A program may use at most 128 MiB of HBM per device.

```python
import jax
import jax.numpy as jnp
from jax import lax

D = 4096
HID = 14336
R = 128
REPLICAS = 4


def block_scale(key, dims, split, low, top_value):
    factor_of, own = 1.0, jax.random.fold_in(key, 6)
    for axis_at, shards_of in split:
        steps = jnp.exp(jax.random.uniform(jax.random.fold_in(own, axis_at), (shards_of,), jnp.float32, low / len(split), top_value / len(split)))
        factor_of = factor_of * jnp.repeat(steps, dims[axis_at] // shards_of).reshape([-1 if axis == axis_at else 1 for axis in range(len(dims))])
    return factor_of


def scatter_about(own_key, extent, spread, bound, pieces=(), dtype=jnp.bfloat16):
    level = block_scale(own_key, extent, pieces, -0.22, 0.18) if pieces else 1.0
    array = jax.random.normal(own_key, extent, jnp.float32) * spread * level
    return jnp.minimum(jnp.maximum(array, -bound), bound).astype(dtype)


def setup_inputs(seed: int = 0) -> dict:
    splits = jax.random.split(jax.random.key(seed), 3)
    return {
        "accumulated": scatter_about(splits[0], (REPLICAS, HID, D), 1.0, 6.0, ((0, 4), (1, 8))),
        "start_q": scatter_about(splits[1], (D, R), 1.0, 6.0, (), jnp.float32),
    }


def reference(accumulated, start_q):
    q_bf = start_q.astype(jnp.bfloat16)

    def left_factor(block):
        return jnp.dot(block.astype(jnp.float32), q_bf.astype(jnp.float32), preferred_element_type=jnp.float32)
    summed_p = jnp.sum(lax.map(left_factor, accumulated), axis=0) / REPLICAS
    gram = jnp.dot(summed_p.T, summed_p, precision=lax.Precision.HIGHEST)
    chol_lower = jnp.linalg.cholesky(gram)
    ortho = lax.linalg.triangular_solve(chol_lower, summed_p, left_side=False, lower=True, transpose_a=True)
    ortho_bf = ortho.astype(jnp.bfloat16)

    def right_factor(block):
        return lax.dot_general(block.astype(jnp.float32), ortho_bf.astype(jnp.float32), (((0,), (0,)), ((), ())), preferred_element_type=jnp.float32)
    new_q = jnp.sum(lax.map(right_factor, accumulated), axis=0) / REPLICAS
    update = lax.dot_general(ortho_bf.astype(jnp.float32), new_q.astype(jnp.bfloat16).astype(jnp.float32), (((1,), (1,)), ((), ())), preferred_element_type=jnp.float32)
    new_error = (accumulated.astype(jnp.float32) - update[None]).astype(jnp.bfloat16)
    return (update, new_error)
```

```python
import functools

import jax
import jax.numpy as jnp
from jax import lax
from jax.experimental import pallas as pl
from jax.experimental.pallas import tpu as pltpu
from jax.sharding import PartitionSpec as P

MESH = pl.DeviceIdType.MESH
HIGHEST = lax.Precision.HIGHEST
VMEM_BYTES = 60 * 1024 * 1024


def chunks_of(rows):
    for count in (14, 7, 8, 4, 2):
        if rows % (16 * count) == 0:
            return count
    return 1


def copy_to(axis, target, src, dst, send_sem, recv_sem):
    return pltpu.make_async_remote_copy(
        src_ref=src, dst_ref=dst, send_sem=send_sem, recv_sem=recv_sem,
        device_id={axis: target}, device_id_type=MESH,
    )


def greet_line(barrier, n, d):
    @pl.when(d > 0)
    def _():
        pl.semaphore_signal(barrier, inc=1, device_id={"dp": d - 1}, device_id_type=MESH)

    @pl.when(d < n - 1)
    def _():
        pl.semaphore_signal(barrier, inc=1, device_id={"dp": d + 1}, device_id_type=MESH)


def line_of(n, d):
    half = n // 2
    left = d < half
    inner = jnp.where(left, d + 1, d - 1)
    outer = jnp.where(left, d - 1, d + 1)
    edge = (d == 0) | (d == n - 1)
    mid = (d == half - 1) | (d == half)
    return inner, outer, edge, mid


def left_kernel(n, count, a_hbm, q_ref, s_ref, zt_ref, gram_ref, a_v, own, part, cross, tot, acc,
                a_sem, in_send, out_send, part_recv, cross_recv, tot_recv):
    rows, wide = a_hbm.shape
    rank = q_ref.shape[1]
    rb = rows // count
    d = lax.axis_index("dp")
    inner, outer, edge, mid = line_of(n, d)

    def at(c):
        return pl.ds(pl.multiple_of(c * rb, rb), rb)

    def load(c):
        return pltpu.make_async_copy(a_hbm.at[at(c)], a_v.at[at(c)], a_sem.at[c])

    def send_part(c):
        return copy_to("dp", inner, own.at[at(c)], part.at[at(c)], in_send.at[c], part_recv.at[c])

    def send_cross(c):
        return copy_to("dp", inner, own.at[at(c)], cross.at[at(c)], in_send.at[c], cross_recv.at[c])

    def send_tot(c):
        return copy_to("dp", outer, tot.at[at(c)], tot.at[at(c)], out_send.at[c], tot_recv.at[c])

    def send_inward(c):
        @pl.when(mid)
        def _():
            send_cross(c).start()

        @pl.when(jnp.logical_not(mid))
        def _():
            send_part(c).start()

    for c in range(count):
        load(c).start()
    barrier = pltpu.get_barrier_semaphore()
    greet_line(barrier, n, d)
    q_bf = q_ref[...].astype(jnp.bfloat16)
    acc[...] = jnp.zeros_like(acc)
    gram_ref[...] = jnp.zeros_like(gram_ref)
    pl.semaphore_wait(barrier, jnp.where(d > 0, 1, 0) + jnp.where(d < n - 1, 1, 0))

    def multiply(c, carry):
        load(c).wait()
        own[at(c), :] = jnp.dot(a_v[at(c), :], q_bf, preferred_element_type=jnp.float32)

        @pl.when(edge)
        def _():
            send_inward(c)

        return carry

    lax.fori_loop(0, count, multiply, 0)
    lag = 1

    def exchange(t, carry):
        @pl.when(jnp.logical_not(edge) & (t < count))
        def _():
            send_part(t).wait_recv()
            own[at(t), :] = own[at(t), :] + part[at(t), :]
            send_inward(t)

        @pl.when(t >= lag)
        def _():
            c = t - lag

            @pl.when(mid)
            def _():
                send_cross(c).wait_recv()
                tot[at(c), :] = own[at(c), :] + cross[at(c), :]

            @pl.when(jnp.logical_not(mid))
            def _():
                send_tot(c).wait_recv()

            @pl.when(jnp.logical_not(edge))
            def _():
                send_tot(c).start()

            mean = tot[at(c), :] / n
            s_ref[at(c), :] = mean
            turned = mean.T
            gram_ref[...] += jnp.dot(turned, mean, precision=HIGHEST, preferred_element_type=jnp.float32)
            high = turned.astype(jnp.bfloat16)
            low = (turned - high.astype(jnp.float32)).astype(jnp.bfloat16)
            both = jnp.concatenate([high, low], axis=0)
            step = 512
            for col in range(0, wide, step):
                acc[:, col:col + step] += jnp.dot(
                    both, a_v[at(c), col:col + step], preferred_element_type=jnp.float32
                )

        return carry

    lax.fori_loop(0, count + lag, exchange, 0)
    for block in range(wide // 128):
        cols = slice(block * 128, block * 128 + 128)
        zt_ref[block * rank:(block + 1) * rank, :] = acc[:rank, cols] + acc[rank:, cols]

    def drain(c, carry):
        send_part(c).wait_send()

        @pl.when(jnp.logical_not(edge))
        def _():
            send_tot(c).wait_send()

        return carry

    lax.fori_loop(0, count, drain, 0)


def eliminate(m_ref, first, last):
    size = m_ref.shape[0]
    row = lax.broadcasted_iota(jnp.int32, (size, size), 0)
    lane = lax.broadcasted_iota(jnp.int32, (size, size), 1)

    def pivot(k, carry):
        m = m_ref[...]
        here = lane == k
        col = jnp.sum(jnp.where(here, m, 0.0), axis=1, keepdims=True)
        line = m_ref[pl.ds(k, 1), :]
        lane1 = lax.broadcasted_iota(jnp.int32, line.shape, 1)
        value = jnp.sum(jnp.where(lane1 == k, line, 0.0), axis=1, keepdims=True)
        below = row > k
        factor = col * (1.0 / value)
        line = jnp.where(lane1 == k, 1.0, line)
        m_ref[...] = jnp.where(below, jnp.where(here, 0.0, m) - factor * line, m)
        return carry

    lax.fori_loop(first, last, pivot, 0)


def right_kernel(n, bits, zt_ref, gram_ref, nq_ref, w_ref, z, got, full, gwork, ggot, m_ref,
                 part, cross, rs_send, rs_recv, ag_send, ag_recv, g_send, g_recv,
                 in_send, out_send, part_recv, cross_recv, tot_recv):
    wide, rank = zt_ref.shape
    d = lax.axis_index("dp")
    me = lax.axis_index("mp")
    inner, outer, edge, mid = line_of(n, d)

    def bit(b):
        return lax.rem(me // (1 << b), 2)

    def partner(b):
        return me + (1 - 2 * bit(b)) * (1 << b)

    barrier = pltpu.get_barrier_semaphore()
    greet_line(barrier, n, d)
    for b in range(bits):
        pl.semaphore_signal(barrier, inc=1, device_id={"mp": partner(b)}, device_id_type=MESH)
    pl.semaphore_wait(barrier, jnp.where(d > 0, 1, 0) + jnp.where(d < n - 1, 1, 0) + bits)

    orders = (tuple(range(bits)), (0,) + tuple(range(bits - 1, 0, -1)))
    length = wide // 2
    offs = [0, length]
    gwork[0] = gram_ref[...]
    spot = 0
    for j in range(bits):
        half = length // 2
        source = zt_ref if j == 0 else z
        copies, keeps = [], []
        for s in range(2):
            b = orders[s][j]
            keeps.append(pl.multiple_of(offs[s] + bit(b) * half, half))
            away = pl.multiple_of(offs[s] + (1 - bit(b)) * half, half)
            copies.append(copy_to(
                "mp", partner(b), source.at[pl.ds(away, half)], got.at[s, pl.ds(spot, half)],
                rs_send.at[s, j], rs_recv.at[s, j],
            ))
        gcopy = copy_to("mp", partner(j), gwork.at[j], ggot.at[j], g_send.at[j], g_recv.at[j])
        gcopy.start()
        for copy in copies:
            copy.start()
        gcopy.wait()
        gwork[j + 1] = gwork[j] + ggot[j]
        for s in range(2):
            copies[s].wait()
            z[pl.ds(keeps[s], half), :] = source[pl.ds(keeps[s], half), :] + got[s, spot:spot + half, :]
        offs = keeps
        spot += half
        length = half
    m_ref[...] = gwork[bits]

    def own(s):
        return z.at[pl.ds(offs[s], length)]

    def tot(s):
        return full.at[pl.ds(offs[s], length)]

    def send_part(s):
        return copy_to("dp", inner, own(s), part.at[s], in_send.at[s], part_recv.at[s])

    def send_cross(s):
        return copy_to("dp", inner, own(s), cross.at[s], in_send.at[s], cross_recv.at[s])

    def send_tot(s):
        return copy_to("dp", outer, tot(s), tot(s), out_send.at[s], tot_recv.at[s])

    def send_inward(s):
        @pl.when(mid)
        def _():
            send_cross(s).start()

        @pl.when(jnp.logical_not(mid))
        def _():
            send_part(s).start()

    for s in range(2):
        @pl.when(jnp.logical_not(edge))
        def _():
            send_part(s).wait_recv()
            own(s)[...] = own(s)[...] + part[s]

        send_inward(s)
    for s in range(2):
        @pl.when(mid)
        def _():
            send_cross(s).wait_recv()
            tot(s)[...] = own(s)[...] + cross[s]

        @pl.when(jnp.logical_not(mid))
        def _():
            send_tot(s).wait_recv()

        @pl.when(jnp.logical_not(edge))
        def _():
            send_tot(s).start()

    done = 0
    for j in range(bits - 1, -1, -1):
        copies = []
        for s in range(2):
            b = orders[s][j]
            mine = full.at[pl.ds(offs[s], length)]
            copies.append(copy_to("mp", partner(b), mine, mine, ag_send.at[s, j], ag_recv.at[s, j]))
        for copy in copies:
            copy.start()
        upto = rank if j == 0 else done + rank // bits
        eliminate(m_ref, done, upto)
        done = upto
        for s in range(2):
            copies[s].wait()
            offs[s] = pl.multiple_of(offs[s] - bit(orders[s][j]) * length, length)
        length *= 2

    m = m_ref[...]
    row = lax.broadcasted_iota(jnp.int32, (rank, rank), 0)
    lane = lax.broadcasted_iota(jnp.int32, (rank, rank), 1)
    pivots = jnp.sum(jnp.where(row == lane, m, 0.0), axis=1, keepdims=True)
    w = jnp.where(lane < row, m, jnp.where(lane == row, 1.0, 0.0)) / jnp.sqrt(pivots)
    w_ref[...] = w

    def turn(block, carry):
        rows = pl.ds(pl.multiple_of(block * rank, rank), rank)
        nq_ref[rows, :] = (
            jnp.dot(w, full[rows, :], precision=HIGHEST, preferred_element_type=jnp.float32) / n
        ).astype(jnp.bfloat16)
        return carry

    lax.fori_loop(0, wide // rank, turn, 0)
    for s in range(2):
        copy_to("dp", inner, part.at[s], part.at[s], in_send.at[s], part_recv.at[s]).wait_send()

        @pl.when(jnp.logical_not(edge))
        def _():
            copy_to("dp", outer, part.at[s], part.at[s], out_send.at[s], tot_recv.at[s]).wait_send()


def last_kernel(a_ref, s_ref, w_ref, nq_ref, update_ref, error_ref):
    rank = w_ref.shape[0]
    ortho = lax.dot_general(
        s_ref[...], w_ref[...], (((1,), (1,)), ((), ())), precision=HIGHEST,
        preferred_element_type=jnp.float32,
    ).astype(jnp.bfloat16)
    group = 4
    for first in range(0, nq_ref.shape[0] // rank, group):
        right = jnp.concatenate(
            [nq_ref[b * rank:(b + 1) * rank, :] for b in range(first, first + group)], axis=1
        )
        cols = slice(first * 128, (first + group) * 128)
        update = jnp.dot(ortho, right, preferred_element_type=jnp.float32)
        update_ref[:, cols] = update
        error_ref[:, cols] = (a_ref[:, cols].astype(jnp.float32) - update).astype(jnp.bfloat16)


def on_device(accumulated, start_q):
    a = accumulated[0]
    rows, wide = a.shape
    rank = start_q.shape[1]
    n, peers = lax.axis_size("dp"), lax.axis_size("mp")
    bits = peers.bit_length() - 1
    assert peers == 1 << bits and n >= 2 and rank == 128
    count = chunks_of(rows)
    f32, bf16 = jnp.float32, jnp.bfloat16
    vmem = pl.BlockSpec(memory_space=pltpu.VMEM)
    dma = pltpu.SemaphoreType.DMA
    summed, zt, gram = pl.pallas_call(
        functools.partial(left_kernel, n, count),
        out_shape=(
            jax.ShapeDtypeStruct((rows, rank), f32),
            jax.ShapeDtypeStruct((wide // 128 * rank, 128), f32),
            jax.ShapeDtypeStruct((rank, rank), f32),
        ),
        in_specs=[pl.BlockSpec(memory_space=pl.ANY), vmem],
        out_specs=(vmem, vmem, vmem),
        scratch_shapes=[
            pltpu.VMEM((rows, wide), bf16),
            pltpu.VMEM((rows, rank), f32),
            pltpu.VMEM((rows, rank), f32),
            pltpu.VMEM((rows, rank), f32),
            pltpu.VMEM((rows, rank), f32),
            pltpu.VMEM((2 * rank, wide), f32),
        ] + [dma((count,))] * 6,
        compiler_params=pltpu.CompilerParams(
            collective_id=0, has_side_effects=True, vmem_limit_bytes=VMEM_BYTES
        ),
        name="left_factor",
    )(a, start_q)
    share = wide // 2 // peers
    new_q, w = pl.pallas_call(
        functools.partial(right_kernel, n, bits),
        out_shape=(
            jax.ShapeDtypeStruct((wide, rank), bf16),
            jax.ShapeDtypeStruct((rank, rank), f32),
        ),
        in_specs=[vmem, vmem],
        out_specs=(vmem, vmem),
        scratch_shapes=[
            pltpu.VMEM((wide, rank), f32),
            pltpu.VMEM((2, wide // 2, rank), f32),
            pltpu.VMEM((wide, rank), f32),
            pltpu.VMEM((bits + 1, rank, rank), f32),
            pltpu.VMEM((bits, rank, rank), f32),
            pltpu.VMEM((rank, rank), f32),
            pltpu.VMEM((2, share, rank), f32),
            pltpu.VMEM((2, share, rank), f32),
        ] + [dma((2, bits))] * 4 + [dma((bits,))] * 2 + [dma((2,))] * 5,
        compiler_params=pltpu.CompilerParams(
            collective_id=1, has_side_effects=True, vmem_limit_bytes=VMEM_BYTES
        ),
        name="right_factor",
    )(zt, gram)
    rb = rows // count
    update, error = pl.pallas_call(
        last_kernel,
        grid=(count,),
        out_shape=(
            jax.ShapeDtypeStruct((rows, wide), f32),
            jax.ShapeDtypeStruct((rows, wide), bf16),
        ),
        in_specs=[
            pl.BlockSpec((rb, wide), lambda i: (i, 0)),
            pl.BlockSpec((rb, rank), lambda i: (i, 0)),
            pl.BlockSpec((rank, rank), lambda i: (0, 0)),
            pl.BlockSpec((wide, rank), lambda i: (0, 0)),
        ],
        out_specs=(
            pl.BlockSpec((rb, wide), lambda i: (i, 0)),
            pl.BlockSpec((rb, wide), lambda i: (i, 0)),
        ),
        name="decompress",
    )(a, summed, w, new_q)
    return (update, error[None])


def solution(mesh):
    placed = (P("dp", "mp", None), P())
    return jax.shard_map(
        on_device,
        mesh=mesh,
        in_specs=placed,
        out_specs=(P("mp", None), P("dp", "mp", None)),
        check_vma=False,
    )
```

```python
import functools

import jax
import jax.numpy as jnp
from jax import lax
from jax.experimental import pallas as pl
from jax.experimental.pallas import tpu as pltpu
from jax.sharding import PartitionSpec as P

MESH = pl.DeviceIdType.MESH
HIGHEST = lax.Precision.HIGHEST
GROUPS = 2
VMEM_BYTES = 60 * 1024 * 1024


def chunks_of(rows):
    for count in (7, 8, 14, 4, 2):
        if rows % (128 * count) == 0:
            return count
    return 1


def copy_to(axis, target, src, dst, send_sem, recv_sem):
    return pltpu.make_async_remote_copy(
        src_ref=src, dst_ref=dst, send_sem=send_sem, recv_sem=recv_sem,
        device_id={axis: target}, device_id_type=MESH,
    )


def greet_line(barrier, n, d):
    @pl.when(d > 0)
    def _():
        pl.semaphore_signal(barrier, inc=1, device_id={"dp": d - 1}, device_id_type=MESH)

    @pl.when(d < n - 1)
    def _():
        pl.semaphore_signal(barrier, inc=1, device_id={"dp": d + 1}, device_id_type=MESH)


def line_of(n, d):
    half = n // 2
    left = d < half
    inner = jnp.where(left, d + 1, d - 1)
    outer = jnp.where(left, d - 1, d + 1)
    edge = (d == 0) | (d == n - 1)
    mid = (d == half - 1) | (d == half)
    return inner, outer, edge, mid


def factors_kernel(n, bits, count, a_hbm, q_ref, s_ref, nq_ref, w_ref, a_v, own, part, cross, acc, z, got,
                   full, gwork, ggot, m_ref, zpart, zcross, a_sem, in_send, out_send, part_recv, cross_recv,
                   tot_recv, rs_send, rs_recv, ag_send, ag_recv, g_send, g_recv, zin_send, zout_send,
                   zpart_recv, zcross_recv, ztot_recv):
    rows, wide = a_hbm.shape
    rank = q_ref.shape[1]
    rg = rank // GROUPS
    rb = rows // count
    blocks = wide // 128
    d = lax.axis_index("dp")
    me = lax.axis_index("mp")
    inner, outer, edge, mid = line_of(n, d)
    tot = s_ref

    def bit(b):
        return lax.rem(me // (1 << b), 2)

    def partner(b):
        return me + (1 - 2 * bit(b)) * (1 << b)

    def load(c):
        some = pl.ds(pl.multiple_of(c * rb, rb), rb)
        return pltpu.make_async_copy(a_hbm.at[some], a_v.at[some], a_sem.at[c])

    def piece(ref, g, c):
        return ref.at[c, g * rg:(g + 1) * rg]

    def send_part(g, c):
        return copy_to("dp", inner, piece(own, g, c), piece(part, g, c), in_send.at[g, c], part_recv.at[g, c])

    def send_cross(g, c):
        return copy_to("dp", inner, piece(own, g, c), piece(cross, g, c), in_send.at[g, c], cross_recv.at[g, c])

    def send_tot(g, c):
        return copy_to("dp", outer, piece(tot, g, c), piece(tot, g, c), out_send.at[g, c], tot_recv.at[g, c])

    def inward(crossing, passing):
        @pl.when(mid)
        def _():
            crossing.start()

        @pl.when(jnp.logical_not(mid))
        def _():
            passing.start()

    for c in range(count):
        load(c).start()
    barrier = pltpu.get_barrier_semaphore()
    greet_line(barrier, n, d)
    for b in range(bits):
        pl.semaphore_signal(barrier, inc=1, device_id={"mp": partner(b)}, device_id_type=MESH)
    q_bf = q_ref[...].astype(jnp.bfloat16)
    gwork[0] = jnp.zeros_like(gwork[0])
    pl.semaphore_wait(barrier, jnp.where(d > 0, 1, 0) + jnp.where(d < n - 1, 1, 0) + bits)

    def multiply(c, carry):
        load(c).wait()
        some = pl.ds(pl.multiple_of(c * rb, rb), rb)
        own[c] = jnp.dot(a_v[some, :], q_bf, preferred_element_type=jnp.float32).T

        @pl.when(edge)
        def _():
            inward(send_cross(0, c), send_part(0, c))

        return carry

    lax.fori_loop(0, count, multiply, 0)

    @pl.when(edge)
    def _():
        for c in range(count):
            inward(send_cross(1, c), send_part(1, c))

    lag = 1

    def exchange(g, t, carry):
        @pl.when(jnp.logical_not(edge) & (t < count))
        def _():
            send_part(g, t).wait_recv()
            mine = piece(own, g, t)
            mine[...] = mine[...] + piece(part, g, t)[...]
            inward(send_cross(g, t), send_part(g, t))

        @pl.when(t >= lag)
        def _():
            c = t - lag

            @pl.when(mid)
            def _():
                send_cross(g, c).wait_recv()
                piece(tot, g, c)[...] = piece(own, g, c)[...] + piece(cross, g, c)[...]

            @pl.when(jnp.logical_not(mid))
            def _():
                send_tot(g, c).wait_recv()

            @pl.when(jnp.logical_not(edge))
            def _():
                send_tot(g, c).start()

            mean = piece(tot, g, c)[...] / n
            high = mean.astype(jnp.bfloat16)
            low = (mean - high.astype(jnp.float32)).astype(jnp.bfloat16)
            both = jnp.concatenate([high, low], axis=0)
            some = pl.ds(pl.multiple_of(c * rb, rb), rb)
            step = 512
            for col in range(0, wide, step):
                acc[g, :, col:col + step] += jnp.dot(
                    both, a_v[some, col:col + step], preferred_element_type=jnp.float32
                )
            if g == GROUPS - 1:
                whole = tot[c] / n
                gwork[0] += lax.dot_general(
                    whole, whole, (((1,), (1,)), ((), ())), precision=HIGHEST,
                    preferred_element_type=jnp.float32,
                )

        return carry

    def run(g, first, last):
        lax.fori_loop(first, last, functools.partial(exchange, g), 0)

    def build(g):
        for block in range(blocks):
            cols = slice(block * 128, block * 128 + 128)
            z[g, block * rg:(block + 1) * rg, :] = acc[g, :rg, cols] + acc[g, rg:, cols]

    orders = (tuple(range(bits)), (0,) + tuple(range(bits - 1, 0, -1)))
    lengths = [blocks * rg // 2 >> j for j in range(bits + 1)]
    offs = []
    for s in range(2):
        at = [s * lengths[0]]
        for j in range(bits):
            at.append(pl.multiple_of(at[j] + bit(orders[s][j]) * lengths[j + 1], lengths[bits]))
        offs.append(at)

    def rs(g, s, j):
        half = lengths[j + 1]
        b = orders[s][j]
        away = pl.multiple_of(offs[s][j] + (1 - bit(b)) * half, lengths[bits])
        spot = lengths[0] - lengths[j]
        return copy_to(
            "mp", partner(b), z.at[g, pl.ds(away, half)], got.at[g, s, spot:spot + half],
            rs_send.at[g, s, j], rs_recv.at[g, s, j],
        )

    def rs_start(g, j):
        for s in range(2):
            rs(g, s, j).start()

    def rs_finish(g, j):
        half, spot = lengths[j + 1], lengths[0] - lengths[j]
        for s in range(2):
            rs(g, s, j).wait()
            keep = pl.ds(offs[s][j + 1], half)
            z[g, keep, :] = z[g, keep, :] + got[g, s, spot:spot + half, :]

    def gram(j):
        return copy_to("mp", partner(j), gwork.at[j], ggot.at[j], g_send.at[j], g_recv.at[j])

    def gram_finish(j):
        gram(j).wait()
        gwork[j + 1] = gwork[j] + ggot[j]

    def share(ref, g, s):
        return ref.at[g, pl.ds(offs[s][bits], lengths[bits])]

    def z_part(g, s):
        return copy_to("dp", inner, share(z, g, s), zpart.at[g, s], zin_send.at[g, s], zpart_recv.at[g, s])

    def z_cross(g, s):
        return copy_to("dp", inner, share(z, g, s), zcross.at[g, s], zin_send.at[g, s], zcross_recv.at[g, s])

    def z_tot(g, s):
        return copy_to("dp", outer, share(full, g, s), share(full, g, s), zout_send.at[g, s], ztot_recv.at[g, s])

    def line_edge(g):
        @pl.when(edge)
        def _():
            for s in range(2):
                inward(z_cross(g, s), z_part(g, s))

    def line_in(g):
        @pl.when(jnp.logical_not(edge))
        def _():
            for s in range(2):
                z_part(g, s).wait_recv()
                mine = share(z, g, s)
                mine[...] = mine[...] + zpart[g, s]
                inward(z_cross(g, s), z_part(g, s))

    def line_out(g):
        for s in range(2):
            @pl.when(mid)
            def _():
                z_cross(g, s).wait_recv()
                share(full, g, s)[...] = share(z, g, s)[...] + zcross[g, s]

            @pl.when(jnp.logical_not(mid))
            def _():
                z_tot(g, s).wait_recv()

            @pl.when(jnp.logical_not(edge))
            def _():
                z_tot(g, s).start()

    def ag(g, s, j):
        mine = full.at[g, pl.ds(offs[s][j + 1], lengths[j + 1])]
        return copy_to("mp", partner(orders[s][j]), mine, mine, ag_send.at[g, s, j], ag_recv.at[g, s, j])

    def ag_start(g, j):
        for s in range(2):
            ag(g, s, j).start()

    def ag_finish(g, j):
        for s in range(2):
            ag(g, s, j).wait()

    acc[...] = jnp.zeros_like(acc)
    run(0, 0, count + lag)
    build(0)
    rs_start(0, 0)
    steps = count + lag
    at = 0
    for j in range(bits):
        upto = steps * (j + 1) // bits
        run(1, at, upto)
        at = upto
        if j < bits - 1:
            rs_finish(0, j)
            rs_start(0, j + 1)
    gram(0).start()
    build(1)
    rs_start(1, 0)
    rs_finish(0, bits - 1)
    line_edge(0)
    for j in range(bits):
        gram_finish(j)
        if j < bits - 1:
            gram(j + 1).start()
        if j == 1:
            line_out(0)
            ag_start(0, bits - 1)
        rs_finish(1, j)
        if j < bits - 1:
            rs_start(1, j + 1)
        if j == 0:
            line_in(0)
    line_edge(1)
    m_ref[...] = gwork[bits]
    portion = rank // 8
    eliminate(m_ref, 0, portion)
    line_in(1)
    ag_finish(0, bits - 1)
    ag_start(0, bits - 2)
    eliminate(m_ref, portion, 2 * portion)
    line_out(1)
    ag_start(1, bits - 1)
    done = 2 * portion
    for j in range(bits - 2, -1, -1):
        upto = rank if j == 0 else done + (rank - done) // (bits - 1)
        eliminate(m_ref, done, upto)
        done = upto
        ag_finish(0, j)
        if j > 0:
            ag_start(0, j - 1)
        ag_finish(1, j + 1)
        ag_start(1, j)

    m = m_ref[...]
    row = lax.broadcasted_iota(jnp.int32, (rank, rank), 0)
    lane = lax.broadcasted_iota(jnp.int32, (rank, rank), 1)
    pivots = jnp.sum(jnp.where(row == lane, m, 0.0), axis=1, keepdims=True)
    w = jnp.where(lane < row, m, jnp.where(lane == row, 1.0, 0.0)) / jnp.sqrt(pivots)
    w_ref[...] = w
    ag_finish(1, 0)

    def turn(block, carry):
        rows_of = pl.ds(pl.multiple_of(block * rg, rg), rg)
        right = jnp.concatenate([full[g, rows_of, :] for g in range(GROUPS)], axis=0)
        nq_ref[pl.ds(pl.multiple_of(block * rank, rank), rank), :] = (
            jnp.dot(w, right, precision=HIGHEST, preferred_element_type=jnp.float32) / n
        ).astype(jnp.bfloat16)
        return carry

    lax.fori_loop(0, blocks, turn, 0)
    for g in range(GROUPS):
        for c in range(count):
            send_part(g, c).wait_send()
        for s in range(2):
            z_part(g, s).wait_send()

        @pl.when(jnp.logical_not(edge))
        def _():
            for c in range(count):
                send_tot(g, c).wait_send()
            for s in range(2):
                z_tot(g, s).wait_send()


def eliminate(m_ref, first, last):
    size = m_ref.shape[0]
    row = lax.broadcasted_iota(jnp.int32, (size, size), 0)
    lane = lax.broadcasted_iota(jnp.int32, (size, size), 1)

    def pivot(k, carry):
        m = m_ref[...]
        here = lane == k
        col = jnp.sum(jnp.where(here, m, 0.0), axis=1, keepdims=True)
        line = m_ref[pl.ds(k, 1), :]
        lane1 = lax.broadcasted_iota(jnp.int32, line.shape, 1)
        value = jnp.sum(jnp.where(lane1 == k, line, 0.0), axis=1, keepdims=True)
        below = row > k
        factor = col * (1.0 / value)
        line = jnp.where(lane1 == k, 1.0, line)
        m_ref[...] = jnp.where(below, jnp.where(here, 0.0, m) - factor * line, m)
        return carry

    lax.fori_loop(first, last, pivot, 0)


def last_kernel(n, a_ref, s_ref, w_ref, nq_ref, update_ref, error_ref):
    rank = w_ref.shape[0]
    ortho = jnp.dot(
        w_ref[...], s_ref[0] / n, precision=HIGHEST, preferred_element_type=jnp.float32
    ).T.astype(jnp.bfloat16)
    group = 4
    for first in range(0, nq_ref.shape[0] // rank, group):
        right = jnp.concatenate(
            [nq_ref[b * rank:(b + 1) * rank, :] for b in range(first, first + group)], axis=1
        )
        cols = slice(first * 128, (first + group) * 128)
        update = jnp.dot(ortho, right, preferred_element_type=jnp.float32)
        update_ref[:, cols] = update
        error_ref[:, cols] = (a_ref[:, cols].astype(jnp.float32) - update).astype(jnp.bfloat16)


def on_device(accumulated, start_q):
    a = accumulated[0]
    rows, wide = a.shape
    rank = start_q.shape[1]
    n, peers = lax.axis_size("dp"), lax.axis_size("mp")
    bits = peers.bit_length() - 1
    assert peers == 1 << bits and bits >= 2 and n >= 2 and rank == 128
    count = chunks_of(rows)
    rb = rows // count
    f32, bf16 = jnp.float32, jnp.bfloat16
    vmem = pl.BlockSpec(memory_space=pltpu.VMEM)
    dma = pltpu.SemaphoreType.DMA
    flat = wide // GROUPS
    summed, new_q, w = pl.pallas_call(
        functools.partial(factors_kernel, n, bits, count),
        out_shape=(
            jax.ShapeDtypeStruct((count, rank, rb), f32),
            jax.ShapeDtypeStruct((wide, rank), bf16),
            jax.ShapeDtypeStruct((rank, rank), f32),
        ),
        in_specs=[pl.BlockSpec(memory_space=pl.ANY), vmem],
        out_specs=(vmem, vmem, vmem),
        scratch_shapes=[
            pltpu.VMEM((rows, wide), bf16),
            pltpu.VMEM((count, rank, rb), f32),
            pltpu.VMEM((count, rank, rb), f32),
            pltpu.VMEM((count, rank, rb), f32),
            pltpu.VMEM((GROUPS, 2 * rank // GROUPS, wide), f32),
            pltpu.VMEM((GROUPS, flat, 128), f32),
            pltpu.VMEM((GROUPS, 2, flat // 2, 128), f32),
            pltpu.VMEM((GROUPS, flat, 128), f32),
            pltpu.VMEM((bits + 1, rank, rank), f32),
            pltpu.VMEM((bits, rank, rank), f32),
            pltpu.VMEM((rank, rank), f32),
            pltpu.VMEM((GROUPS, 2, flat // 2 // peers, 128), f32),
            pltpu.VMEM((GROUPS, 2, flat // 2 // peers, 128), f32),
            dma((count,)),
        ] + [dma((GROUPS, count))] * 5 + [dma((GROUPS, 2, bits))] * 4 + [dma((bits,))] * 2
        + [dma((GROUPS, 2))] * 5,
        compiler_params=pltpu.CompilerParams(
            collective_id=0, has_side_effects=True, vmem_limit_bytes=VMEM_BYTES
        ),
        name="factors",
    )(a, start_q)
    split = 2 if rb % 256 == 0 else 1
    small = rb // split
    update, error = pl.pallas_call(
        functools.partial(last_kernel, n),
        grid=(count, split),
        out_shape=(
            jax.ShapeDtypeStruct((rows, wide), f32),
            jax.ShapeDtypeStruct((rows, wide), bf16),
        ),
        in_specs=[
            pl.BlockSpec((small, wide), lambda i, j: (i * split + j, 0)),
            pl.BlockSpec((1, rank, small), lambda i, j: (i, 0, j)),
            pl.BlockSpec((rank, rank), lambda i, j: (0, 0)),
            pl.BlockSpec((wide, rank), lambda i, j: (0, 0)),
        ],
        out_specs=(
            pl.BlockSpec((small, wide), lambda i, j: (i * split + j, 0)),
            pl.BlockSpec((small, wide), lambda i, j: (i * split + j, 0)),
        ),
        name="decompress",
    )(a, summed, w, new_q)
    return (update, error[None])


def solution(mesh):
    placed = (P("dp", "mp", None), P())
    return jax.shard_map(
        on_device,
        mesh=mesh,
        in_specs=placed,
        out_specs=(P("mp", None), P("dp", "mp", None)),
        check_vma=False,
    )
```

```python
import functools

import jax
import jax.numpy as jnp
from jax import lax
from jax.experimental import pallas as pl
from jax.experimental.pallas import tpu as pltpu
from jax.sharding import PartitionSpec as P

MESH = pl.DeviceIdType.MESH
HIGHEST = lax.Precision.HIGHEST
GROUPS = 2
BLOCK = 256
VMEM_BYTES = 60 * 1024 * 1024


def chunks_of(rows):
    for count in (7, 8, 14, 4, 2):
        if rows % (128 * count) == 0:
            return count
    return 1


def copy_to(axis, target, src, dst, send_sem, recv_sem):
    return pltpu.make_async_remote_copy(
        src_ref=src, dst_ref=dst, send_sem=send_sem, recv_sem=recv_sem,
        device_id={axis: target}, device_id_type=MESH,
    )


def greet_line(barrier, n, d):
    @pl.when(d > 0)
    def _():
        pl.semaphore_signal(barrier, inc=1, device_id={"dp": d - 1}, device_id_type=MESH)

    @pl.when(d < n - 1)
    def _():
        pl.semaphore_signal(barrier, inc=1, device_id={"dp": d + 1}, device_id_type=MESH)


def line_of(n, d):
    half = n // 2
    left = d < half
    inner = jnp.where(left, d + 1, d - 1)
    outer = jnp.where(left, d - 1, d + 1)
    edge = (d == 0) | (d == n - 1)
    mid = (d == half - 1) | (d == half)
    return inner, outer, edge, mid


def factors_kernel(n, bits, count, a_hbm, q_ref, ortho_ref, nq_ref, a_v, tot, own, part, cross, acc, z, got,
                   full, gwork, ggot, m_ref, zpart, zcross, a_sem, in_send, out_send, part_recv, cross_recv,
                   tot_recv, rs_send, rs_recv, ag_send, ag_recv, g_send, g_recv, zin_send, zout_send,
                   zpart_recv, zcross_recv, ztot_recv):
    rows, wide = a_hbm.shape
    rank = q_ref.shape[1]
    rg = rank // GROUPS
    rb = rows // count
    blocks = wide // 128
    d = lax.axis_index("dp")
    me = lax.axis_index("mp")
    inner, outer, edge, mid = line_of(n, d)

    def bit(b):
        return lax.rem(me // (1 << b), 2)

    def partner(b):
        return me + (1 - 2 * bit(b)) * (1 << b)

    def load(c):
        some = pl.ds(pl.multiple_of(c * rb, rb), rb)
        return pltpu.make_async_copy(a_hbm.at[some], a_v.at[some], a_sem.at[c])

    def piece(ref, g, c):
        return ref.at[c, pl.ds(pl.multiple_of(g * rg, rg), rg)]

    def send_part(g, c):
        return copy_to("dp", inner, piece(own, g, c), piece(part, g, c), in_send.at[g, c], part_recv.at[g, c])

    def send_cross(g, c):
        return copy_to("dp", inner, piece(own, g, c), piece(cross, g, c), in_send.at[g, c], cross_recv.at[g, c])

    def send_tot(g, c):
        return copy_to("dp", outer, piece(tot, g, c), piece(tot, g, c), out_send.at[g, c], tot_recv.at[g, c])

    def inward(crossing, passing):
        @pl.when(mid)
        def _():
            crossing.start()

        @pl.when(jnp.logical_not(mid))
        def _():
            passing.start()

    for c in range(count):
        load(c).start()
    barrier = pltpu.get_barrier_semaphore()
    greet_line(barrier, n, d)
    for b in range(bits):
        pl.semaphore_signal(barrier, inc=1, device_id={"mp": partner(b)}, device_id_type=MESH)
    q_bf = q_ref[...].astype(jnp.bfloat16)
    gwork[0] = jnp.zeros_like(gwork[0])
    pl.semaphore_wait(barrier, jnp.where(d > 0, 1, 0) + jnp.where(d < n - 1, 1, 0) + bits)

    def multiply(c, carry):
        load(c).wait()
        some = pl.ds(pl.multiple_of(c * rb, rb), rb)
        own[c] = jnp.dot(a_v[some, :], q_bf, preferred_element_type=jnp.float32).T

        @pl.when(edge)
        def _():
            inward(send_cross(0, c), send_part(0, c))

        return carry

    lax.fori_loop(0, count, multiply, 0)

    @pl.when(edge)
    def _():
        for c in range(count):
            inward(send_cross(1, c), send_part(1, c))

    lag = 2
    total = GROUPS * count

    def exchange(t, carry):
        @pl.when(jnp.logical_not(edge) & (t < total))
        def _():
            g, c = t // count, lax.rem(t, count)
            send_part(g, c).wait_recv()
            mine = piece(own, g, c)
            mine[...] = mine[...] + piece(part, g, c)[...]
            inward(send_cross(g, c), send_part(g, c))

        @pl.when(t >= lag)
        def _():
            g, c = (t - lag) // count, lax.rem(t - lag, count)

            @pl.when(mid)
            def _():
                send_cross(g, c).wait_recv()
                piece(tot, g, c)[...] = piece(own, g, c)[...] + piece(cross, g, c)[...]

            @pl.when(jnp.logical_not(mid))
            def _():
                send_tot(g, c).wait_recv()

            @pl.when(jnp.logical_not(edge))
            def _():
                send_tot(g, c).start()

            mean = piece(tot, g, c)[...] / n
            high = mean.astype(jnp.bfloat16)
            low = (mean - high.astype(jnp.float32)).astype(jnp.bfloat16)
            both = jnp.concatenate([high, low], axis=0)
            some = pl.ds(pl.multiple_of(c * rb, rb), rb)
            step = 512
            for col in range(0, wide, step):
                acc[g, :, col:col + step] += jnp.dot(
                    both, a_v[some, col:col + step], preferred_element_type=jnp.float32
                )

            @pl.when(g == GROUPS - 1)
            def _():
                whole = tot[c] / n
                gwork[0] += lax.dot_general(
                    whole, whole, (((1,), (1,)), ((), ())), precision=HIGHEST,
                    preferred_element_type=jnp.float32,
                )

        return carry

    def run(first, last):
        lax.fori_loop(first, last, exchange, 0)

    def build(g):
        for block in range(blocks):
            cols = slice(block * 128, block * 128 + 128)
            z[g, block * rg:(block + 1) * rg, :] = acc[g, :rg, cols] + acc[g, rg:, cols]

    orders = (tuple(range(bits)), (0,) + tuple(range(bits - 1, 0, -1)))
    lengths = [blocks * rg // 2 >> j for j in range(bits + 1)]
    offs = []
    for s in range(2):
        at = [s * lengths[0]]
        for j in range(bits):
            at.append(pl.multiple_of(at[j] + bit(orders[s][j]) * lengths[j + 1], lengths[bits]))
        offs.append(at)

    def rs(g, s, j):
        half = lengths[j + 1]
        b = orders[s][j]
        away = pl.multiple_of(offs[s][j] + (1 - bit(b)) * half, lengths[bits])
        spot = lengths[0] - lengths[j]
        return copy_to(
            "mp", partner(b), z.at[g, pl.ds(away, half)], got.at[g, s, spot:spot + half],
            rs_send.at[g, s, j], rs_recv.at[g, s, j],
        )

    def rs_start(g, j):
        for s in range(2):
            rs(g, s, j).start()

    def rs_finish(g, j):
        half, spot = lengths[j + 1], lengths[0] - lengths[j]
        for s in range(2):
            rs(g, s, j).wait()
            keep = pl.ds(offs[s][j + 1], half)
            z[g, keep, :] = z[g, keep, :] + got[g, s, spot:spot + half, :]

    def gram(j):
        return copy_to("mp", partner(j), gwork.at[j], ggot.at[j], g_send.at[j], g_recv.at[j])

    def gram_finish(j):
        gram(j).wait()
        gwork[j + 1] = gwork[j] + ggot[j]

    def share(ref, g, s):
        return ref.at[g, pl.ds(offs[s][bits], lengths[bits])]

    def z_part(g, s):
        return copy_to("dp", inner, share(z, g, s), zpart.at[g, s], zin_send.at[g, s], zpart_recv.at[g, s])

    def z_cross(g, s):
        return copy_to("dp", inner, share(z, g, s), zcross.at[g, s], zin_send.at[g, s], zcross_recv.at[g, s])

    def z_tot(g, s):
        return copy_to("dp", outer, share(full, g, s), share(full, g, s), zout_send.at[g, s], ztot_recv.at[g, s])

    def line_edge(g):
        @pl.when(edge)
        def _():
            for s in range(2):
                inward(z_cross(g, s), z_part(g, s))

    def line_in(g):
        @pl.when(jnp.logical_not(edge))
        def _():
            for s in range(2):
                z_part(g, s).wait_recv()
                mine = share(z, g, s)
                mine[...] = mine[...] + zpart[g, s]
                inward(z_cross(g, s), z_part(g, s))

    def line_out(g):
        for s in range(2):
            @pl.when(mid)
            def _():
                z_cross(g, s).wait_recv()
                share(full, g, s)[...] = share(z, g, s)[...] + zcross[g, s]

            @pl.when(jnp.logical_not(mid))
            def _():
                z_tot(g, s).wait_recv()

            @pl.when(jnp.logical_not(edge))
            def _():
                z_tot(g, s).start()

    def ag(g, s, j):
        mine = full.at[g, pl.ds(offs[s][j + 1], lengths[j + 1])]
        return copy_to("mp", partner(orders[s][j]), mine, mine, ag_send.at[g, s, j], ag_recv.at[g, s, j])

    def ag_start(g, j):
        for s in range(2):
            ag(g, s, j).start()

    def ag_finish(g, j):
        for s in range(2):
            ag(g, s, j).wait()

    acc[...] = jnp.zeros_like(acc)
    run(0, count + lag)
    build(0)
    rs_start(0, 0)
    at = count + lag
    for j in range(bits):
        upto = count + lag + count * (j + 1) // bits
        run(at, upto)
        at = upto
        if j < bits - 1:
            rs_finish(0, j)
            rs_start(0, j + 1)
    gram(0).start()
    build(1)
    rs_start(1, 0)
    rs_finish(0, bits - 1)
    line_edge(0)
    for j in range(bits):
        gram_finish(j)
        if j < bits - 1:
            gram(j + 1).start()
        if j == 1:
            line_out(0)
            ag_start(0, bits - 1)
        rs_finish(1, j)
        if j < bits - 1:
            rs_start(1, j + 1)
        if j == 0:
            line_in(0)
    line_edge(1)
    m_ref[...] = gwork[bits]
    portion = rank // 8
    eliminate(m_ref, 0, portion)
    line_in(1)
    ag_finish(0, bits - 1)
    ag_start(0, bits - 2)
    eliminate(m_ref, portion, 2 * portion)
    line_out(1)
    ag_start(1, bits - 1)
    done = 2 * portion
    for j in range(bits - 2, -1, -1):
        upto = rank if j == 0 else done + (rank - done) // (bits - 1)
        eliminate(m_ref, done, upto)
        done = upto
        ag_finish(0, j)
        if j > 0:
            ag_start(0, j - 1)
        ag_finish(1, j + 1)
        ag_start(1, j)

    m = m_ref[...]
    row = lax.broadcasted_iota(jnp.int32, (rank, rank), 0)
    lane = lax.broadcasted_iota(jnp.int32, (rank, rank), 1)
    pivots = jnp.sum(jnp.where(row == lane, m, 0.0), axis=1, keepdims=True)
    w = jnp.where(lane < row, m, jnp.where(lane == row, 1.0, 0.0)) / jnp.sqrt(pivots)

    def straighten(c, carry):
        ortho_ref[pl.ds(pl.multiple_of(c * rb, rb), rb), :] = jnp.dot(
            w, tot[c] / n, precision=HIGHEST, preferred_element_type=jnp.float32
        ).T.astype(jnp.bfloat16)
        return carry

    lax.fori_loop(0, count, straighten, 0)
    ag_finish(1, 0)

    def turn(block, carry):
        rows_of = pl.ds(pl.multiple_of(block * rg, rg), rg)
        right = jnp.concatenate([full[g, rows_of, :] for g in range(GROUPS)], axis=0)
        nq_ref[pl.ds(pl.multiple_of(block * rank, rank), rank), :] = (
            jnp.dot(w, right, precision=HIGHEST, preferred_element_type=jnp.float32) / n
        ).astype(jnp.bfloat16)
        return carry

    lax.fori_loop(0, blocks, turn, 0)
    for g in range(GROUPS):
        for c in range(count):
            send_part(g, c).wait_send()
        for s in range(2):
            z_part(g, s).wait_send()

        @pl.when(jnp.logical_not(edge))
        def _():
            for c in range(count):
                send_tot(g, c).wait_send()
            for s in range(2):
                z_tot(g, s).wait_send()


def eliminate(m_ref, first, last):
    size = m_ref.shape[0]
    row = lax.broadcasted_iota(jnp.int32, (size, size), 0)
    lane = lax.broadcasted_iota(jnp.int32, (size, size), 1)

    def pivot(k, carry):
        m = m_ref[...]
        here = lane == k
        col = jnp.sum(jnp.where(here, m, 0.0), axis=1, keepdims=True)
        line = m_ref[pl.ds(k, 1), :]
        lane1 = lax.broadcasted_iota(jnp.int32, line.shape, 1)
        value = jnp.sum(jnp.where(lane1 == k, line, 0.0), axis=1, keepdims=True)
        below = row > k
        factor = col * (1.0 / value)
        line = jnp.where(lane1 == k, 1.0, line)
        m_ref[...] = jnp.where(below, jnp.where(here, 0.0, m) - factor * line, m)
        return carry

    lax.fori_loop(first, last, pivot, 0)


def last_kernel(a_ref, ortho_ref, nq_ref, update_ref, error_ref):
    rank = ortho_ref.shape[1]
    ortho = ortho_ref[...]
    group = 4
    for first in range(0, nq_ref.shape[0] // rank, group):
        right = jnp.concatenate(
            [nq_ref[b * rank:(b + 1) * rank, :] for b in range(first, first + group)], axis=1
        )
        cols = slice(first * 128, (first + group) * 128)
        update = jnp.dot(ortho, right, preferred_element_type=jnp.float32)
        update_ref[:, cols] = update
        error_ref[:, cols] = (a_ref[:, cols].astype(jnp.float32) - update).astype(jnp.bfloat16)


def on_device(accumulated, start_q):
    a = accumulated[0]
    rows, wide = a.shape
    rank = start_q.shape[1]
    n, peers = lax.axis_size("dp"), lax.axis_size("mp")
    bits = peers.bit_length() - 1
    assert peers == 1 << bits and bits >= 2 and n >= 2 and rank == 128
    count = chunks_of(rows)
    rb = rows // count
    f32, bf16 = jnp.float32, jnp.bfloat16
    vmem = pl.BlockSpec(memory_space=pltpu.VMEM)
    dma = pltpu.SemaphoreType.DMA
    flat = wide // GROUPS
    ortho, new_q = pl.pallas_call(
        functools.partial(factors_kernel, n, bits, count),
        out_shape=(
            jax.ShapeDtypeStruct((rows, rank), bf16),
            jax.ShapeDtypeStruct((wide, rank), bf16),
        ),
        in_specs=[pl.BlockSpec(memory_space=pl.ANY), vmem],
        out_specs=(vmem, vmem),
        scratch_shapes=[
            pltpu.VMEM((rows, wide), bf16),
            pltpu.VMEM((count, rank, rb), f32),
            pltpu.VMEM((count, rank, rb), f32),
            pltpu.VMEM((count, rank, rb), f32),
            pltpu.VMEM((count, rank, rb), f32),
            pltpu.VMEM((GROUPS, 2 * rank // GROUPS, wide), f32),
            pltpu.VMEM((GROUPS, flat, 128), f32),
            pltpu.VMEM((GROUPS, 2, flat // 2, 128), f32),
            pltpu.VMEM((GROUPS, flat, 128), f32),
            pltpu.VMEM((bits + 1, rank, rank), f32),
            pltpu.VMEM((bits, rank, rank), f32),
            pltpu.VMEM((rank, rank), f32),
            pltpu.VMEM((GROUPS, 2, flat // 2 // peers, 128), f32),
            pltpu.VMEM((GROUPS, 2, flat // 2 // peers, 128), f32),
            dma((count,)),
        ] + [dma((GROUPS, count))] * 5 + [dma((GROUPS, 2, bits))] * 4 + [dma((bits,))] * 2
        + [dma((GROUPS, 2))] * 5,
        compiler_params=pltpu.CompilerParams(
            collective_id=0, has_side_effects=True, vmem_limit_bytes=VMEM_BYTES
        ),
        name="factors",
    )(a, start_q)
    small = BLOCK if rows % BLOCK == 0 else rb
    update, error = pl.pallas_call(
        last_kernel,
        grid=(rows // small,),
        out_shape=(
            jax.ShapeDtypeStruct((rows, wide), f32),
            jax.ShapeDtypeStruct((rows, wide), bf16),
        ),
        in_specs=[
            pl.BlockSpec((small, wide), lambda i: (i, 0)),
            pl.BlockSpec((small, rank), lambda i: (i, 0)),
            pl.BlockSpec((wide, rank), lambda i: (0, 0)),
        ],
        out_specs=(
            pl.BlockSpec((small, wide), lambda i: (i, 0)),
            pl.BlockSpec((small, wide), lambda i: (i, 0)),
        ),
        name="decompress",
    )(a, ortho, new_q)
    return (update, error[None])


def solution(mesh):
    placed = (P("dp", "mp", None), P())
    return jax.shard_map(
        on_device,
        mesh=mesh,
        in_specs=placed,
        out_specs=(P("mp", None), P("dp", "mp", None)),
        check_vma=False,
    )
```
